128 devices in a mesh: row: 8 (over x_hi, y), col: 16 (over z, x_lo, core).
Axes of the slice: x: 4 (x_hi: 2, x_lo: 2; x = x_hi * 2 + x_lo), y: 4, z: 4, core: 2. Of those that a mesh axis runs over, the one named last changes fastest.
Arguments:
- fields: bfloat16 [128, 128, 1024], P('row', 'col'), may hold values from -6 to 6
- cotangent: bfloat16 [128, 128, 1024], P('row', 'col'), may hold values from -6 to 6
- query_weight: bfloat16 [1024, 1024], P(('row', 'col')), may hold values from -1 to 6
- key_weight: bfloat16 [1024, 1024], P(('row', 'col')), may hold values from -1 to 6
- value_weight: bfloat16 [1024, 1024], P(('row', 'col')), may hold values from -0.1875 to 0.1875
- output_weight: bfloat16 [1024, 1024], P(('row', 'col')), may hold values from -0.1875 to 0.1875
- expert_ids: int32 [8, 16, 128, 2], P('row', 'col'), may hold values from 0 to 31, all different within a row; in each aligned block of 128 rows (0 to 127, 128 to 255, ..., all dimensions but the last counted through in order) at most 10 rows name the same one
- gate_values: float32 [8, 16, 128, 2], P('row', 'col'), may hold values from 0.2 to 1
- gate_weight: bfloat16 [128, 1024, 1024], P(('row', 'col')), may hold values from -0.1875 to 0.1875
- up_weight: bfloat16 [128, 1024, 1024], P(('row', 'col')), may hold values from -0.1875 to 0.1875
- down_weight: bfloat16 [128, 1024, 1024], P(('row', 'col')), may hold values from -0.09375 to 0.09375
Outputs:
- field_grad: bfloat16 [128, 128, 1024], P('row', 'col')
- gate_grad: bfloat16 [128, 1024, 1024], P(('row', 'col'))
- up_grad: bfloat16 [128, 1024, 1024], P(('row', 'col'))
- down_grad: bfloat16 [128, 1024, 1024], P(('row', 'col'))
The draws below stay inside these ranges and needn't reach their ends.
Inputs may be any that keep to these rules, and one draw needn't show every extreme that they name: `expert_ids`: the 2 entries of a cell differ; among one device's 128 cells no expert is named more than 10 times, a bound that some block reaches.
All inputs are finite; a program needn't handle non-finite values.
Results may differ from the reference program's by a relative error of at most 0.0095.
Values may be sent and summed in bfloat16 or wider, within the bound.
No kernel may reach another device: no remote copies, remote signals or barrier semaphores. Data moves between devices by JAX's collectives and lax.ppermute only.
A program may use at most 192 MiB of HBM per device.

```python
import math
import jax
import jax.numpy as jnp
import numpy as np
from jax import lax

D = 1024
HEADS = 16
FF = 4096
EXPERTS = 32
TOP = 2
TPS = 4
SLICE = 1024
H = 128
W = 128
TOK_DEV = 128
TOKENS = 16384
CAP = 10
N_ROW = 8
N_COL = 16


def shared_projection(key, which):
    base = jax.random.truncated_normal(jax.random.fold_in(key, 101 + which), -4.0, 4.0, (D, D), jnp.float32) * D ** (-0.5)
    return base.astype(jnp.bfloat16)


def draw_query_weight(key, part):
    return shared_projection(key, 0)


def draw_key_weight(key, part):
    return shared_projection(key, 1)


def block_levels(rng, shape, pieces, least, largest):
    def one(position, parts):
        draws = jax.random.uniform(jax.random.fold_in(jax.random.fold_in(rng, 6), position), (parts,), jnp.float32, least / len(pieces), largest / len(pieces))
        return jnp.repeat(jnp.exp(draws), shape[position] // parts).reshape((-1,) + (1,) * (len(shape) - position - 1))

    level = one(*pieces[0])
    for cut in pieces[1:]:
        level = level * one(*cut)
    return level


def deal_out(own_key, own, number, rows, amount, top, reach, slope):
    ranking = jax.random.permutation(own_key, amount)
    crowded, ordinary = shares(amount, rows * top, reach, slope, True), shares(amount, rows * top, reach, slope, False)
    places = jnp.arange(amount)

    def named(tallies, turn):
        used = int((tallies > 0).sum())
        fixed = max(1, used // 4)
        passed = fixed + (places - fixed + turn * (used - fixed)) % max(1, amount - fixed)
        return jnp.zeros((amount,), jnp.int32).at[ranking[jnp.where(places < fixed, places, passed)]].set(jnp.asarray(tallies, jnp.int32))

    tallies = jnp.where(number % 4 == 0, named(crowded, number // 4), named(ordinary, number - number // 4 - 1))
    mixed = jax.random.permutation(jax.random.fold_in(own, 3), amount)
    source_of, sink = mixed[0:amount // 2 * 2:2], mixed[1:amount // 2 * 2:2]
    margin = jnp.minimum(tallies[source_of] - 1, reach - tallies[sink]) // 2
    margin = jnp.where((source_of == ranking[0]) | (sink == ranking[0]) | (tallies[sink] == 0), 0, jnp.maximum(margin, 0))
    passed = jax.random.randint(jax.random.fold_in(own, 4), (amount // 2,), 0, 1 << 20) % (margin + 1)
    tallies = tallies.at[source_of].add(-passed).at[sink].add(passed)
    labels = jnp.searchsorted(jnp.cumsum(tallies), jnp.arange(rows * top), side="right").astype(jnp.int32)
    table = labels.reshape(top, rows).T
    table = table[jax.random.permutation(jax.random.fold_in(own, 1), rows)]
    turn = jax.random.randint(jax.random.fold_in(own, 2), (rows, 1), 0, top)
    return jnp.take_along_axis(table, (jnp.arange(top)[None, :] + turn) % top, axis=1)


def shares(number_of, total, reach, skew, full):
    portions = [(1 << 20) // math.isqrt(grade ** skew) + 1 for grade in range(1, number_of + 1)]
    largest = reach if full else min(reach, max(-(-total // number_of), total * portions[0] // sum(portions)))
    least = 1 if total - largest >= number_of - 1 else 0
    counts, spare = [largest] + [least] * (number_of - 1), total - largest - least * (number_of - 1)
    while spare > 0:
        free = [i for i in range(1, number_of) if counts[i] < largest] or [i for i in range(1, number_of) if counts[i] < reach]
        pool, left = sum([portions[i] for i in free]), spare
        for i in free:
            extra = min(reach - counts[i], max(1, left * portions[i] // pool), spare)
            counts[i] = counts[i] + extra
            spare = spare - extra
    return np.array(counts)


def normal_values(rng, shape, deviation, bound, split=(), kind=jnp.bfloat16):
    gain = block_levels(rng, shape, split, -0.22, 0.18) if split else 1.0
    drawn = jax.random.normal(rng, shape, jnp.float32) * deviation * gain
    return jnp.minimum(jnp.maximum(drawn, -bound), bound).astype(kind)


def setup_inputs(seed: int = 0) -> dict:
    arg_keys = jax.random.split(jax.random.key(seed), 12)
    fields = normal_values(arg_keys[0], (H, W, D), 1.0, 6.0, ((0, 8), (1, 16)))
    cotangent = normal_values(arg_keys[1], (H, W, D), 1.0, 6.0, ((0, 8), (1, 16)))
    query_weight = draw_query_weight(jax.random.fold_in(arg_keys[11], 71), 0)
    key_weight = draw_key_weight(jax.random.fold_in(arg_keys[11], 71), 0)
    value_weight = normal_values(arg_keys[4], (D, D), D ** -0.5, 0.1875, ((0, 128),))
    output_weight = normal_values(arg_keys[5], (D, D), D ** -0.5, 0.1875, ((0, 128),))
    expert_ids_keys = jax.random.split(jax.random.fold_in(arg_keys[6], 1), N_ROW * N_COL * TOK_DEV // TOK_DEV)
    expert_ids_turns = jax.random.permutation(jax.random.fold_in(arg_keys[6], 3), N_ROW * N_COL * TOK_DEV // TOK_DEV)
    expert_ids = jax.vmap(lambda own, number: deal_out(jax.random.fold_in(arg_keys[6], 2), own, number, TOK_DEV, EXPERTS, TOP, CAP, 2))(expert_ids_keys, expert_ids_turns).reshape((N_ROW, N_COL, TOK_DEV, TOP))
    gate_values = jnp.clip(0.2 + 0.8 * jax.random.uniform(arg_keys[7], (N_ROW, N_COL, TOK_DEV, TOP), jnp.float32) ** block_levels(arg_keys[7], (N_ROW, N_COL, TOK_DEV, TOP), ((0, 8), (1, 16)), -0.2, 0.2), 0.2, 1.0)
    gate_weight = normal_values(arg_keys[8], (EXPERTS * TPS, D, SLICE), D ** -0.5, 0.1875, ((0, 128),))
    up_weight = normal_values(arg_keys[9], (EXPERTS * TPS, D, SLICE), D ** -0.5, 0.1875, ((0, 128),))
    down_weight = normal_values(arg_keys[10], (EXPERTS * TPS, SLICE, D), FF ** -0.5, 0.09375, ((0, 128),))
    return {"fields": fields, "cotangent": cotangent, "query_weight": query_weight, "key_weight": key_weight, "value_weight": value_weight, "output_weight": output_weight, "expert_ids": expert_ids, "gate_values": gate_values, "gate_weight": gate_weight, "up_weight": up_weight, "down_weight": down_weight}


EPS = 1e-06

def normalize(values):
    scale = lax.rsqrt(lax.optimization_barrier(jnp.mean(values * values, axis=-1, keepdims=True)) + EPS)
    return (values * scale, scale)

def norm_back(grads, normed, scale):
    return scale * (grads - normed * lax.optimization_barrier(jnp.mean(grads * normed, axis=-1, keepdims=True)))

def expand(first, second, form):
    return jnp.einsum(form, first.astype(jnp.float32), second.astype(jnp.float32))

def attention_forward(normed_half, query_weight, key_weight, value_weight, output_weight):
    latitudes, longitudes, features = normed_half.shape
    head_size = features // HEADS
    flat_rows = normed_half.reshape(latitudes * longitudes, features)

    def project(weight):
        result = jnp.dot(flat_rows, weight, preferred_element_type=jnp.float32)
        return result.astype(jnp.bfloat16).reshape(latitudes, longitudes, HEADS, head_size)
    queries = project(query_weight)
    key_rows = project(key_weight)
    value_rows = project(value_weight)
    factor = 1.0 / math.sqrt(head_size)
    scores = expand(queries, key_rows, 'bqhd,bkhd->bhqk') * factor
    attention = jax.nn.softmax(scores, axis=-1)
    attention_half = attention.astype(jnp.bfloat16)
    attended = expand(attention_half, value_rows, 'bhqk,bkhd->bqhd').astype(jnp.bfloat16)
    mixture = jnp.dot(attended.reshape(latitudes * longitudes, features), output_weight, preferred_element_type=jnp.float32)
    return (mixture, (queries, key_rows, value_rows, attention, attention_half))

def attention_backward(block_half, stored, query_weight, key_weight, value_weight, output_weight):
    queries, key_rows, value_rows, attention, attention_half = stored
    latitudes, longitudes, head_count, head_size = queries.shape
    features = head_count * head_size
    factor = 1.0 / math.sqrt(head_size)
    out_grad = jnp.dot(block_half.reshape(-1, features), output_weight.T, preferred_element_type=jnp.float32)
    out_grad = out_grad.astype(jnp.bfloat16).reshape(latitudes, longitudes, head_count, head_size)
    mass_grad = expand(out_grad, value_rows, 'bqhd,bkhd->bhqk')
    score_grad = attention * (mass_grad - lax.optimization_barrier(jnp.sum(attention * mass_grad, axis=-1, keepdims=True))) * factor
    score_grad = score_grad.astype(jnp.bfloat16)
    query_grad = expand(score_grad, key_rows, 'bhqk,bkhd->bqhd').astype(jnp.bfloat16)
    key_grad = expand(score_grad, queries, 'bhqk,bqhd->bkhd').astype(jnp.bfloat16)
    value_grad = expand(attention_half, out_grad, 'bhqk,bqhd->bkhd').astype(jnp.bfloat16)

    def through(grads, weight):
        return jnp.dot(grads.reshape(-1, features), weight.T, preferred_element_type=jnp.float32)
    return through(query_grad, query_weight) + through(key_grad, key_weight) + through(value_grad, value_weight)

def expert_terms(inputs, mix_grad, gate_block, up_block, down_block):
    gate_pre = jnp.dot(inputs, gate_block, preferred_element_type=jnp.float32)
    up_pre = jnp.dot(inputs, up_block, preferred_element_type=jnp.float32)
    sigmoid_gate = jax.nn.sigmoid(gate_pre)
    swish_gate = gate_pre * sigmoid_gate
    hidden = (swish_gate * up_pre).astype(jnp.bfloat16)
    hidden_grad = jnp.dot(mix_grad, down_block.T, preferred_element_type=jnp.float32)
    gate_delta = (hidden_grad * up_pre * sigmoid_gate * (1.0 + gate_pre * (1.0 - sigmoid_gate))).astype(jnp.bfloat16)
    up_delta = (hidden_grad * swish_gate).astype(jnp.bfloat16)
    down_term = jnp.dot(hidden.T, mix_grad, preferred_element_type=jnp.float32).astype(jnp.bfloat16)
    gate_term = jnp.dot(inputs.T, gate_delta, preferred_element_type=jnp.float32).astype(jnp.bfloat16)
    up_term = jnp.dot(inputs.T, up_delta, preferred_element_type=jnp.float32).astype(jnp.bfloat16)
    returned = jnp.dot(gate_delta, gate_block.T, preferred_element_type=jnp.float32)
    returned = returned + jnp.dot(up_delta, up_block.T, preferred_element_type=jnp.float32)
    return (gate_term, up_term, down_term, returned)

def assignment_slots(chosen):
    onehot = (chosen[:, None] == jnp.arange(EXPERTS, dtype=jnp.int32)[None, :]).astype(jnp.int32)
    before = jnp.cumsum(onehot, axis=0) - onehot
    return lax.optimization_barrier(jnp.sum(before * onehot, axis=1)).astype(jnp.int32)

def reference(fields, cotangent, query_weight, key_weight, value_weight, output_weight, expert_ids, gate_values, gate_weight, up_weight, down_weight):
    device_count = N_ROW * N_COL
    fields_full = fields.astype(jnp.float32)
    normed_in, scale_in = normalize(fields_full)
    normed_in_half = normed_in.astype(jnp.bfloat16)
    mixture, stored = attention_forward(normed_in_half, query_weight, key_weight, value_weight, output_weight)
    mid_stream = (fields_full.reshape(-1, D) + mixture).astype(jnp.bfloat16)
    normed_mid, scale_mid = normalize(mid_stream.astype(jnp.float32))
    normed_mid_half = normed_mid.astype(jnp.bfloat16)
    chosen = expert_ids.reshape(device_count, TOK_DEV * TOP)
    slot_index = jax.vmap(assignment_slots)(chosen)
    owner = jnp.arange(device_count, dtype=jnp.int32)[:, None]
    places = ((chosen * device_count + owner) * CAP + slot_index).reshape(-1).astype(jnp.int32)
    cotangent_full = cotangent.reshape(TOKENS, D).astype(jnp.float32)
    weights = gate_values.reshape(TOKENS, TOP)
    mix_grad = (weights[:, :, None] * cotangent_full[:, None, :]).astype(jnp.bfloat16).reshape(TOKENS * TOP, D)
    inputs = jnp.broadcast_to(normed_mid_half[:, None, :], (TOKENS, TOP, D)).reshape(TOKENS * TOP, D)
    blank_buffer = jnp.zeros((EXPERTS * device_count * CAP, D), jnp.bfloat16)
    send_inputs = blank_buffer.at[places].set(inputs).reshape(EXPERTS, device_count * CAP, D)
    send_grads = blank_buffer.at[places].set(mix_grad).reshape(EXPERTS, device_count * CAP, D)
    gate_full = gate_weight.reshape(EXPERTS, TPS, D, SLICE).transpose(0, 2, 1, 3).reshape(EXPERTS, D, FF)
    up_full = up_weight.reshape(EXPERTS, TPS, D, SLICE).transpose(0, 2, 1, 3).reshape(EXPERTS, D, FF)
    down_full = down_weight.reshape(EXPERTS, FF, D)

    def one_expert(operands):
        return expert_terms(*operands)
    gate_term, up_term, down_term, returned = lax.map(one_expert, (send_inputs, send_grads, gate_full, up_full, down_full))
    gathered = returned.reshape(-1, D)[places]
    normed_grad = lax.optimization_barrier(jnp.sum(gathered.reshape(TOKENS, TOP, D), axis=1))
    block_grad = cotangent_full + norm_back(normed_grad, normed_mid, scale_mid)
    block_half = block_grad.astype(jnp.bfloat16)
    branch_grad = attention_backward(block_half.reshape(H, W, D), stored, query_weight, key_weight, value_weight, output_weight)
    field_total = block_grad + norm_back(branch_grad, normed_in.reshape(-1, D), scale_in.reshape(-1, 1))
    field_grad = field_total.astype(jnp.bfloat16).reshape(H, W, D)
    gate_grad = gate_term.reshape(EXPERTS, D, TPS, SLICE).transpose(0, 2, 1, 3).reshape(EXPERTS * TPS, D, SLICE)
    up_grad = up_term.reshape(EXPERTS, D, TPS, SLICE).transpose(0, 2, 1, 3).reshape(EXPERTS * TPS, D, SLICE)
    down_grad = down_term.reshape(EXPERTS * TPS, SLICE, D)
    return (field_grad, gate_grad, up_grad, down_grad)
```

```python
import math

import jax
import jax.numpy as jnp
from jax import lax
from jax.sharding import PartitionSpec as P

HEADS = 16
EXPERTS = 32
CAP = 10


EPS = 1e-06
ROW = ("xh", "y")
COL = ("z", "xl", "core")
SAME_CORE = ("xh", "y", "z", "xl")
EVERY = ("xh", "y", "z", "xl", "core")


def normalize(values):
    scale = lax.rsqrt(jnp.mean(values * values, axis=-1, keepdims=True) + EPS)
    return (values * scale, scale)


def norm_back(grads, normed, scale):
    return scale * (grads - normed * jnp.mean(grads * normed, axis=-1, keepdims=True))


def contract_rows(left, right):
    return lax.dot_general(
        left, right, (((0,), (0,)), ((), ())), preferred_element_type=jnp.float32
    )


def times_transposed(left, right):
    return lax.dot_general(
        left, right, (((1,), (1,)), ((), ())), preferred_element_type=jnp.float32
    )


def attention_forward(normed_half, query_weight, key_weight, value_weight, output_weight):
    latitudes, longitudes, features = normed_half.shape
    head_size = features // HEADS
    flat_rows = normed_half.reshape(latitudes * longitudes, features)

    def project(weight):
        result = jnp.dot(flat_rows, weight, preferred_element_type=jnp.float32)
        return result.astype(jnp.bfloat16).reshape(latitudes, longitudes, HEADS, head_size)

    queries = project(query_weight)
    key_rows = project(key_weight)
    value_rows = project(value_weight)
    factor = 1.0 / math.sqrt(head_size)
    scores = (
        jnp.einsum("bqhd,bkhd->bhqk", queries, key_rows, preferred_element_type=jnp.float32)
        * factor
    )
    attention = jax.nn.softmax(scores, axis=-1)
    attention_half = attention.astype(jnp.bfloat16)
    attended = jnp.einsum(
        "bhqk,bkhd->bqhd", attention_half, value_rows, preferred_element_type=jnp.float32
    ).astype(jnp.bfloat16)
    mixture = jnp.dot(
        attended.reshape(latitudes * longitudes, features),
        output_weight,
        preferred_element_type=jnp.float32,
    )
    return (mixture, (queries, key_rows, value_rows, attention, attention_half))


def attention_backward(block_half, stored, query_weight, key_weight, value_weight, output_weight):
    queries, key_rows, value_rows, attention, attention_half = stored
    latitudes, longitudes, head_count, head_size = queries.shape
    features = head_count * head_size
    factor = 1.0 / math.sqrt(head_size)
    out_grad = times_transposed(block_half.reshape(-1, features), output_weight)
    out_grad = out_grad.astype(jnp.bfloat16).reshape(latitudes, longitudes, head_count, head_size)
    mass_grad = jnp.einsum(
        "bqhd,bkhd->bhqk", out_grad, value_rows, preferred_element_type=jnp.float32
    )
    score_grad = (
        attention * (mass_grad - jnp.sum(attention * mass_grad, axis=-1, keepdims=True)) * factor
    )
    score_grad = score_grad.astype(jnp.bfloat16)
    query_grad = jnp.einsum(
        "bhqk,bkhd->bqhd", score_grad, key_rows, preferred_element_type=jnp.float32
    ).astype(jnp.bfloat16)
    key_grad = jnp.einsum(
        "bhqk,bqhd->bkhd", score_grad, queries, preferred_element_type=jnp.float32
    ).astype(jnp.bfloat16)
    value_grad = jnp.einsum(
        "bhqk,bqhd->bkhd", attention_half, out_grad, preferred_element_type=jnp.float32
    ).astype(jnp.bfloat16)
    total = times_transposed(query_grad.reshape(-1, features), query_weight)
    total = total + times_transposed(key_grad.reshape(-1, features), key_weight)
    return total + times_transposed(value_grad.reshape(-1, features), value_weight)


def expert_terms(inputs, mix_grad, gate_block, up_block, down_block):
    gate_pre = jnp.dot(inputs, gate_block, preferred_element_type=jnp.float32)
    up_pre = jnp.dot(inputs, up_block, preferred_element_type=jnp.float32)
    sigmoid_gate = jax.nn.sigmoid(gate_pre)
    swish_gate = gate_pre * sigmoid_gate
    hidden = (swish_gate * up_pre).astype(jnp.bfloat16)
    hidden_grad = times_transposed(mix_grad, down_block)
    gate_delta = (
        hidden_grad * up_pre * sigmoid_gate * (1.0 + gate_pre * (1.0 - sigmoid_gate))
    ).astype(jnp.bfloat16)
    up_delta = (hidden_grad * swish_gate).astype(jnp.bfloat16)
    down_term = contract_rows(hidden, mix_grad).astype(jnp.bfloat16)
    gate_term = contract_rows(inputs, gate_delta).astype(jnp.bfloat16)
    up_term = contract_rows(inputs, up_delta).astype(jnp.bfloat16)
    returned = times_transposed(gate_delta, gate_block) + times_transposed(up_delta, up_block)
    return (gate_term, up_term, down_term, returned)


def assignment_slots(chosen):
    onehot = (chosen[:, None] == jnp.arange(EXPERTS, dtype=jnp.int32)[None, :]).astype(jnp.int32)
    before = jnp.cumsum(onehot, axis=0) - onehot
    return jnp.sum(before * onehot, axis=1)


def gather_weights(*shards):
    rows, features = shards[0].shape
    mine = jnp.stack(shards)
    peers = lax.axis_size(SAME_CORE)
    spread = jnp.broadcast_to(mine[None], (peers,) + mine.shape)
    own = lax.all_to_all(spread, SAME_CORE, split_axis=0, concat_axis=0, tiled=True)
    other = lax.ppermute(own, "core", [(0, 1), (1, 0)])
    first = lax.axis_index("core") == 0
    low = jnp.where(first, own, other)
    high = jnp.where(first, other, own)
    both = jnp.stack([low, high], axis=2)
    return [both[:, which].reshape(-1, features) for which in range(len(shards))]


def body(
    fields,
    cotangent,
    query_weight,
    key_weight,
    value_weight,
    output_weight,
    expert_ids,
    gate_values,
    gate_weight,
    up_weight,
    down_weight,
):
    field_rows, cotangent_rows = (
        lax.all_to_all(fields, COL, split_axis=0, concat_axis=1, tiled=True),
        lax.all_to_all(cotangent, COL, split_axis=0, concat_axis=1, tiled=True),
    )
    query_all, key_all, value_all, output_all = gather_weights(
        query_weight, key_weight, value_weight, output_weight
    )
    latitudes, longitudes, features = field_rows.shape
    token_count = latitudes * longitudes
    top_count = expert_ids.shape[-1]
    fields_full = field_rows.astype(jnp.float32)
    normed_in, scale_in = normalize(fields_full)
    normed_in_half = normed_in.astype(jnp.bfloat16)
    mixture, stored = attention_forward(normed_in_half, query_all, key_all, value_all, output_all)
    mid_stream = (fields_full.reshape(token_count, features) + mixture).astype(jnp.bfloat16)
    normed_mid, scale_mid = normalize(mid_stream.astype(jnp.float32))
    normed_mid_half = normed_mid.astype(jnp.bfloat16)
    chosen = expert_ids.reshape(token_count * top_count)
    slot_index = assignment_slots(chosen)
    places = chosen * CAP + slot_index
    cotangent_full = cotangent_rows.reshape(token_count, features).astype(jnp.float32)
    weights = gate_values.reshape(token_count, top_count)
    mix_grad = (
        (weights[:, :, None] * cotangent_full[:, None, :])
        .astype(jnp.bfloat16)
        .reshape(token_count * top_count, features)
    )
    inputs = jnp.broadcast_to(
        normed_mid_half[:, None, :], (token_count, top_count, features)
    ).reshape(token_count * top_count, features)
    blank_buffer = jnp.zeros((EXPERTS * CAP, features), jnp.bfloat16)
    send_inputs = blank_buffer.at[places].set(inputs)
    send_grads = blank_buffer.at[places].set(mix_grad)
    all_devices = lax.axis_size(EVERY)
    slice_count = all_devices // EXPERTS

    def spread(buffer):
        widened = jnp.broadcast_to(
            buffer.reshape(EXPERTS, 1, CAP, features), (EXPERTS, slice_count, CAP, features)
        )
        return widened.reshape(all_devices, CAP, features)

    recv_inputs, recv_grads = (
        lax.all_to_all(
            spread(send_inputs), EVERY, split_axis=0, concat_axis=0, tiled=True
        ),
        lax.all_to_all(spread(send_grads), EVERY, split_axis=0, concat_axis=0, tiled=True),
    )
    row_count = all_devices * CAP
    gate_term, up_term, down_term, returned = expert_terms(
        recv_inputs.reshape(row_count, features),
        recv_grads.reshape(row_count, features),
        gate_weight[0],
        up_weight[0],
        down_weight[0],
    )
    coming_back = lax.all_to_all(
        returned.reshape(all_devices, CAP, features).astype(jnp.bfloat16),
        EVERY,
        split_axis=0,
        concat_axis=0,
        tiled=True,
    ).astype(jnp.float32)
    summed = jnp.sum(coming_back.reshape(EXPERTS, slice_count, CAP, features), axis=1)
    gathered = summed.reshape(EXPERTS * CAP, features)[places]
    normed_grad = jnp.sum(gathered.reshape(token_count, top_count, features), axis=1)
    block_grad = cotangent_full + norm_back(normed_grad, normed_mid, scale_mid)
    block_half = block_grad.astype(jnp.bfloat16)
    branch_grad = attention_backward(
        block_half.reshape(latitudes, longitudes, features),
        stored,
        query_all,
        key_all,
        value_all,
        output_all,
    )
    field_total = block_grad + norm_back(
        branch_grad, normed_in.reshape(token_count, features), scale_in.reshape(token_count, 1)
    )
    field_half = field_total.astype(jnp.bfloat16).reshape(latitudes, longitudes, features)
    field_grad = lax.all_to_all(field_half, COL, split_axis=1, concat_axis=0, tiled=True)
    return (field_grad, gate_term[None], up_term[None], down_term[None])


def solution(mesh):
    fine = jax.sharding.Mesh(mesh.devices.reshape(2, 4, 4, 2, 2), EVERY)
    in_specs = (
        P(ROW, COL, None),
        P(ROW, COL, None),
        P(EVERY, None),
        P(EVERY, None),
        P(EVERY, None),
        P(EVERY, None),
        P(ROW, COL, None, None),
        P(ROW, COL, None, None),
        P(EVERY, None, None),
        P(EVERY, None, None),
        P(EVERY, None, None),
    )
    out_specs = (
        P(ROW, COL, None),
        P(EVERY, None, None),
        P(EVERY, None, None),
        P(EVERY, None, None),
    )
    return jax.shard_map(body, mesh=fine, in_specs=in_specs, out_specs=out_specs, check_vma=False)
```

```python
import math

import jax
import jax.numpy as jnp
from jax import lax
from jax.experimental import pallas as pl
from jax.experimental.pallas import tpu as pltpu
from jax.sharding import PartitionSpec as P

HEADS = 16
EXPERTS = 32
CAP = 10
MAIN = 8
EPS = 1e-06
LANES = 128
ROW = ("xh", "y")
COL = ("z", "xl", "core")
SAME_CORE = ("xh", "y", "z", "xl")
EVERY = ("xh", "y", "z", "xl", "core")
SWAP = [(0, 1), (1, 0)]
BF16 = jnp.bfloat16
F32 = jnp.float32
ANYWHERE = pl.BlockSpec(memory_space=pl.ANY)
IN_VMEM = pl.BlockSpec(memory_space=pltpu.VMEM)
IN_SMEM = pl.BlockSpec(memory_space=pltpu.SMEM)
PARAMS = pltpu.CompilerParams(vmem_limit_bytes=58 << 20)


def dot_nn(left, right):
    return lax.dot_general(left, right, (((1,), (0,)), ((), ())), preferred_element_type=F32)


def dot_nt(left, right):
    return lax.dot_general(left, right, (((1,), (1,)), ((), ())), preferred_element_type=F32)


def dot_tn(left, right):
    return lax.dot_general(left, right, (((0,), (0,)), ((), ())), preferred_element_type=F32)


def normalize(values):
    scale = lax.rsqrt(jnp.mean(values * values, axis=-1, keepdims=True) + EPS)
    return (values * scale, scale)


def norm_back(grads, normed, scale):
    return scale * (grads - normed * jnp.mean(grads * normed, axis=-1, keepdims=True))


def weight_copies(core_ref, own_ref, other_ref, weights, sems):
    core = core_ref[0]
    copies = []
    for which in range(4):
        copies.append(
            (
                pltpu.make_async_copy(
                    own_ref.at[:, which], weights.at[which, :, core], sems.at[which, 0]
                ),
                pltpu.make_async_copy(
                    other_ref.at[:, which], weights.at[which, :, 1 - core], sems.at[which, 1]
                ),
            )
        )
    return copies


def wait_for(copies, which):
    for copy in copies[which]:
        copy.wait()


def whole(weights, which):
    return weights[which].reshape(1024, 1024)


def lane_halves():
    return lax.broadcasted_iota(jnp.int32, (1, LANES), 1) < 64


def split_heads(pair, low):
    zero = jnp.zeros_like(pair)
    return jnp.concatenate([jnp.where(low, pair, zero), jnp.where(low, zero, pair)], axis=0)


def pack_blocks(rows, overflow, groups, write):
    main = groups * MAIN
    for chunk in range(8):
        lanes = slice(chunk * LANES, (chunk + 1) * LANES)
        write(chunk * 8, 8, rows[:main, lanes].reshape(groups, 8, LANES).astype(BF16))
        overflow[:, chunk, :] = rows[main:, lanes]
    write(64, 16, overflow[...].reshape(groups, 16, LANES).astype(BF16))


def forward_kernel(
    core_ref,
    place_ref,
    gate_ref,
    rows_ref,
    own_ref,
    other_ref,
    send_ref,
    query_ref,
    key_ref,
    value_ref,
    probs_ref,
    mid_ref,
    weights,
    overflow,
    sems,
):
    copies = weight_copies(core_ref, own_ref, other_ref, weights, sems)
    for pair in copies:
        for copy in pair:
            copy.start()
    low = lane_halves()
    fields = rows_ref[:, 0:8, :].astype(F32).reshape(128, 1024)
    normed, _ = normalize(fields)
    normed = normed.astype(BF16)
    for which, out in enumerate((query_ref, key_ref, value_ref)):
        wait_for(copies, which)
        out[...] = dot_nn(normed, whole(weights, which)).astype(BF16)
    attended = []
    for block in range(8):
        lanes = slice(block * LANES, (block + 1) * LANES)
        scores = dot_nt(query_ref[:, lanes], split_heads(key_ref[:, lanes], low)) * 0.125
        parts = []
        for half in range(2):
            part = scores[:, half * LANES : (half + 1) * LANES]
            part = jnp.exp(part - jnp.max(part, axis=-1, keepdims=True))
            parts.append(part / jnp.sum(part, axis=-1, keepdims=True))
        probs = jnp.concatenate(parts, axis=1)
        probs_ref[block] = probs
        attended.append(
            dot_nn(probs.astype(BF16), split_heads(value_ref[:, lanes], low)).astype(BF16)
        )
    wait_for(copies, 3)
    mixture = dot_nn(jnp.concatenate(attended, axis=1), whole(weights, 3))
    mid = (fields + mixture).astype(BF16)
    mid_ref[...] = mid
    normed_mid, _ = normalize(mid.astype(F32))
    slot = lax.broadcasted_iota(jnp.int32, (EXPERTS * CAP, 128), 0)
    first = slot == place_ref[0:1, :]
    second = slot == place_ref[1:2, :]
    zero = jnp.zeros((EXPERTS * CAP, 128), F32)
    gate = jnp.where(first, gate_ref[0:1, :], zero) + jnp.where(second, gate_ref[1:2, :], zero)
    gate = jnp.sum(gate, axis=1, keepdims=True)
    select = (jnp.where(first, 1.0, zero) + jnp.where(second, 1.0, zero)).astype(BF16)
    inputs = dot_nn(select, normed_mid.astype(BF16))

    def write(base):
        def put(start, size, block):
            for copy in range(2):
                send_ref[:, copy, base + start : base + start + size, :] = block

        return put

    pack_blocks(inputs, overflow, EXPERTS, write(0))
    cotangent = rows_ref[:, 8:16, :].astype(F32).reshape(128, 1024).astype(BF16)
    grads = gate * dot_nn(select, cotangent)
    pack_blocks(grads, overflow, EXPERTS, write(80))


def unpack_kernel(own_ref, other_ref, inputs_ref, grads_ref, overflow):
    for base, out in ((0, inputs_ref), (80, grads_ref)):
        for half, source in enumerate((own_ref, other_ref)):
            start = half * 640
            overflow[...] = (
                source[:, base + 64 : base + 80, :].astype(F32).reshape(128, 8, LANES)
            )
            for chunk in range(8):
                lanes = slice(chunk * LANES, (chunk + 1) * LANES)
                tile = source[:, base + chunk * 8 : base + chunk * 8 + 8, :]
                out[start : start + 512, lanes] = (
                    tile.astype(F32).reshape(512, LANES).astype(BF16)
                )
                out[start + 512 : start + 640, lanes] = overflow[:, chunk, :].astype(BF16)


def return_kernel(own_ref, other_ref, send_ref, overflow):
    def put(start, size, block):
        send_ref[:, start : start + size, :] = block

    pack_blocks(own_ref[...].astype(F32) + other_ref[...].astype(F32), overflow, 64, put)


def backward_kernel(
    core_ref,
    place_ref,
    back_ref,
    rows_ref,
    own_ref,
    other_ref,
    query_ref,
    key_ref,
    value_ref,
    probs_ref,
    mid_ref,
    out_ref,
    weights,
    returned,
    overflow,
    grad_query,
    grad_key,
    grad_value,
    sems,
):
    copies = weight_copies(core_ref, own_ref, other_ref, weights, sems)
    for which in (3, 0, 1, 2):
        for copy in copies[which]:
            copy.start()
    low = lane_halves()
    for copy in range(2):
        start = copy * 320
        overflow[...] = back_ref[:, copy, 64:80, :].astype(F32).reshape(64, 8, LANES)
        for chunk in range(8):
            lanes = slice(chunk * LANES, (chunk + 1) * LANES)
            tile = back_ref[:, copy, chunk * 8 : chunk * 8 + 8, :]
            returned[start : start + 256, lanes] = (
                tile.astype(F32).reshape(256, LANES).astype(BF16)
            )
            returned[start + 256 : start + 320, lanes] = overflow[:, chunk, :].astype(BF16)
    slot = lax.broadcasted_iota(jnp.int32, (128, EXPERTS * CAP), 1)
    zero = jnp.zeros((128, EXPERTS * CAP), F32)
    select = jnp.where(slot == place_ref[:, 0:1], 1.0, zero) + jnp.where(
        slot == place_ref[:, 1:2], 1.0, zero
    )
    select = select.astype(BF16)
    normed_grad = dot_nn(select, returned[0:320, :]) + dot_nn(select, returned[320:640, :])
    normed_mid, scale_mid = normalize(mid_ref[...].astype(F32))
    cotangent = rows_ref[:, 8:16, :].astype(F32).reshape(128, 1024)
    block_grad = cotangent + norm_back(normed_grad, normed_mid, scale_mid)
    wait_for(copies, 3)
    out_grad = dot_nt(block_grad.astype(BF16), whole(weights, 3)).astype(BF16)
    for block in range(8):
        lanes = slice(block * LANES, (block + 1) * LANES)
        outs = out_grad[:, lanes]
        probs = probs_ref[block]
        mass = probs * dot_nt(outs, split_heads(value_ref[:, lanes], low))
        parts = []
        for half in range(2):
            part = slice(half * LANES, (half + 1) * LANES)
            total = jnp.sum(mass[:, part], axis=-1, keepdims=True)
            parts.append((mass[:, part] - probs[:, part] * total) * 0.125)
        score_grad = jnp.concatenate(parts, axis=1).astype(BF16)
        grad_query[:, lanes] = dot_nn(score_grad, split_heads(key_ref[:, lanes], low)).astype(BF16)
        keys = dot_tn(score_grad, query_ref[:, lanes])
        grad_key[:, lanes] = jnp.where(low, keys[0:128], keys[128:256]).astype(BF16)
        values = dot_tn(probs.astype(BF16), outs)
        grad_value[:, lanes] = jnp.where(low, values[0:128], values[128:256]).astype(BF16)
    wait_for(copies, 0)
    branch = dot_nt(grad_query[...], whole(weights, 0))
    wait_for(copies, 1)
    branch = branch + dot_nt(grad_key[...], whole(weights, 1))
    wait_for(copies, 2)
    branch = branch + dot_nt(grad_value[...], whole(weights, 2))
    fields = rows_ref[:, 0:8, :].astype(F32).reshape(128, 1024)
    normed, scale = normalize(fields)
    total = block_grad + norm_back(branch, normed, scale)
    out_ref[...] = total.reshape(16, 8, 1024).astype(BF16)


def shape(*dims, dtype=BF16):
    return jax.ShapeDtypeStruct(dims, dtype)


def forward(core, places, gates, rows, own, other):
    return pl.pallas_call(
        forward_kernel,
        out_shape=(
            shape(EXPERTS, 2, 160, LANES),
            shape(128, 1024),
            shape(128, 1024),
            shape(128, 1024),
            shape(8, 128, 256, dtype=F32),
            shape(128, 1024),
        ),
        in_specs=[IN_SMEM, IN_VMEM, IN_VMEM, IN_VMEM, ANYWHERE, ANYWHERE],
        out_specs=tuple([IN_VMEM] * 6),
        scratch_shapes=[
            pltpu.VMEM((4, 64, 2, 8, 1024), BF16),
            pltpu.VMEM((64, 8, LANES), F32),
            pltpu.SemaphoreType.DMA((4, 2)),
        ],
        compiler_params=PARAMS,
        name="forward",
    )(core, places, gates, rows, own, other)


def unpack(own, other):
    return pl.pallas_call(
        unpack_kernel,
        out_shape=(shape(1280, 1024), shape(1280, 1024)),
        in_specs=[IN_VMEM, IN_VMEM],
        out_specs=(IN_VMEM, IN_VMEM),
        scratch_shapes=[pltpu.VMEM((128, 8, LANES), F32)],
        compiler_params=PARAMS,
        name="unpack",
    )(own, other)


def pack_return(own, other):
    return pl.pallas_call(
        return_kernel,
        out_shape=shape(64, 80, LANES),
        in_specs=[IN_VMEM, IN_VMEM],
        out_specs=IN_VMEM,
        scratch_shapes=[pltpu.VMEM((128, 8, LANES), F32)],
        compiler_params=PARAMS,
        name="pack_return",
    )(own, other)


def backward(core, places, back, rows, own, other, stored):
    return pl.pallas_call(
        backward_kernel,
        out_shape=shape(16, 8, 1024),
        in_specs=[IN_SMEM, IN_VMEM, IN_VMEM, IN_VMEM, ANYWHERE, ANYWHERE] + [IN_VMEM] * 5,
        out_specs=IN_VMEM,
        scratch_shapes=[
            pltpu.VMEM((4, 64, 2, 8, 1024), BF16),
            pltpu.VMEM((640, 1024), BF16),
            pltpu.VMEM((64, 8, LANES), F32),
            pltpu.VMEM((128, 1024), BF16),
            pltpu.VMEM((128, 1024), BF16),
            pltpu.VMEM((128, 1024), BF16),
            pltpu.SemaphoreType.DMA((4, 2)),
        ],
        compiler_params=PARAMS,
        name="backward",
    )(core, places, back, rows, own, other, *stored)


def expert_terms(inputs, mix_grad, gate_block, up_block, down_block):
    half = inputs.shape[0] // 2
    gate_pre = dot_nn(inputs, gate_block)
    up_pre = dot_nn(inputs, up_block)
    sigmoid_gate = jax.nn.sigmoid(gate_pre)
    swish_gate = gate_pre * sigmoid_gate
    hidden = (swish_gate * up_pre).astype(BF16)
    hidden_grad = dot_nt(mix_grad, down_block)
    gate_delta = (
        hidden_grad * up_pre * sigmoid_gate * (1.0 + gate_pre * (1.0 - sigmoid_gate))
    ).astype(BF16)
    up_delta = (hidden_grad * swish_gate).astype(BF16)

    def returned(part):
        return dot_nt(gate_delta[part], gate_block) + dot_nt(up_delta[part], up_block)

    away = lax.ppermute(returned(slice(half, None)).astype(BF16), "core", SWAP)
    kept = returned(slice(0, half))
    down_term = dot_tn(hidden, mix_grad).astype(BF16)
    gate_term = dot_tn(inputs, gate_delta).astype(BF16)
    up_term = dot_tn(inputs, up_delta).astype(BF16)
    return (gate_term, up_term, down_term, kept, away)


def assignment_places(chosen):
    onehot = (chosen[:, None] == jnp.arange(EXPERTS, dtype=jnp.int32)[None, :]).astype(jnp.int32)
    before = jnp.cumsum(onehot, axis=0) - onehot
    slot = jnp.sum(before * onehot, axis=1)
    over = EXPERTS * MAIN + chosen * (CAP - MAIN) + slot - MAIN
    return jnp.where(slot < MAIN, chosen * MAIN + slot, over)


def body(
    fields,
    cotangent,
    query_weight,
    key_weight,
    value_weight,
    output_weight,
    expert_ids,
    gate_values,
    gate_weight,
    up_weight,
    down_weight,
):
    mine = jnp.stack([query_weight, key_weight, value_weight, output_weight])
    spread = jnp.broadcast_to(mine[None], (64,) + mine.shape)
    own = lax.all_to_all(spread, SAME_CORE, split_axis=0, concat_axis=0, tiled=True)
    other = lax.ppermute(own, "core", SWAP)
    both = jnp.concatenate([fields, cotangent], axis=1)
    rows = lax.all_to_all(both, COL, split_axis=0, concat_axis=0, tiled=True)
    core = lax.axis_index("core").astype(jnp.int32).reshape(1)
    places = assignment_places(expert_ids.reshape(256)).reshape(128, 2)
    gates = gate_values.reshape(128, 2)
    send, *stored = forward(core, places.T, gates.T, rows, own, other)
    arrived = lax.all_to_all(
        send.reshape(64, 160, LANES), SAME_CORE, split_axis=0, concat_axis=0, tiled=True
    )
    partner = lax.ppermute(arrived, "core", SWAP)
    inputs, grads = unpack(arrived, partner)
    gate_term, up_term, down_term, kept, away = expert_terms(
        inputs, grads, gate_weight[0], up_weight[0], down_weight[0]
    )
    send_back = pack_return(kept, away)
    back = lax.all_to_all(send_back, SAME_CORE, split_axis=0, concat_axis=0, tiled=True)
    field_half = backward(
        core, places, back.reshape(EXPERTS, 2, 80, LANES), rows, own, other, stored
    )
    field_grad = lax.all_to_all(field_half, COL, split_axis=0, concat_axis=0, tiled=True)
    return (field_grad, gate_term[None], up_term[None], down_term[None])


def solution(mesh):
    fine = jax.sharding.Mesh(mesh.devices.reshape(2, 4, 4, 2, 2), EVERY)
    in_specs = (
        P(ROW, COL, None),
        P(ROW, COL, None),
        P(EVERY, None),
        P(EVERY, None),
        P(EVERY, None),
        P(EVERY, None),
        P(ROW, COL, None, None),
        P(ROW, COL, None, None),
        P(EVERY, None, None),
        P(EVERY, None, None),
        P(EVERY, None, None),
    )
    out_specs = (
        P(ROW, COL, None),
        P(EVERY, None, None),
        P(EVERY, None, None),
        P(EVERY, None, None),
    )
    return jax.shard_map(body, mesh=fine, in_specs=in_specs, out_specs=out_specs, check_vma=False)
```

```python
import jax
import jax.numpy as jnp
from jax import lax
from jax.experimental import pallas as pl
from jax.experimental.pallas import tpu as pltpu
from jax.sharding import PartitionSpec as P

EXPERTS = 32
CAP = 10
MAIN = 8
EPS = 1e-06
LANES = 128
ROW = ("xh", "y")
COL = ("z", "xl", "core")
SAME_CORE = ("xh", "y", "z", "xl")
BACKWARD_GRANT = 60
EVERY = ("xh", "y", "z", "xl", "core")
SWAP = [(0, 1), (1, 0)]
BF16 = jnp.bfloat16
F32 = jnp.float32
ANYWHERE = pl.BlockSpec(memory_space=pl.ANY)
IN_VMEM = pl.BlockSpec(memory_space=pltpu.VMEM)
IN_HBM = pl.BlockSpec(memory_space=pltpu.HBM)
IN_SMEM = pl.BlockSpec(memory_space=pltpu.SMEM)


def grant(mebibytes):
    return pltpu.CompilerParams(vmem_limit_bytes=mebibytes << 20)


def dot_nn(left, right):
    return lax.dot_general(left, right, (((1,), (0,)), ((), ())), preferred_element_type=F32)


def dot_nt(left, right):
    return lax.dot_general(left, right, (((1,), (1,)), ((), ())), preferred_element_type=F32)


def dot_tn(left, right):
    return lax.dot_general(left, right, (((0,), (0,)), ((), ())), preferred_element_type=F32)


def normalize(values):
    scale = lax.rsqrt(jnp.mean(values * values, axis=-1, keepdims=True) + EPS)
    return (values * scale, scale)


def norm_back(grads, normed, scale):
    return scale * (grads - normed * jnp.mean(grads * normed, axis=-1, keepdims=True))


def weight_copies(place, pieces, weights, sems):
    core, halves = place[0], (place[1], place[2], place[3], place[1])
    copies = [[], [], [], []]
    for other in range(2):
        arrived, *neighbours = pieces[other * 5 : other * 5 + 5]
        row = core if other == 0 else 1 - core
        for which in range(4):
            for half in range(2):
                source = neighbours[which] if half else arrived.at[:, which]
                side = 1 - halves[which] if half else halves[which]
                lanes = pl.ds(pl.multiple_of(side * 512, 512), 512)
                copies[which].append(
                    pltpu.make_async_copy(
                        source,
                        weights.at[which, :, row, :, lanes],
                        sems.at[which, other * 2 + half],
                    )
                )
    return copies


def wait_for(copies, which):
    for copy in copies[which]:
        copy.wait()


def whole(weights, which):
    return weights[which].reshape(1024, 1024)


def lane_halves():
    return lax.broadcasted_iota(jnp.int32, (1, LANES), 1) < 64


def split_heads(pair, low):
    zero = jnp.zeros_like(pair)
    return jnp.concatenate([jnp.where(low, pair, zero), jnp.where(low, zero, pair)], axis=0)


def pack_blocks(rows, overflow, groups, write):
    main = groups * MAIN
    for chunk in range(8):
        lanes = slice(chunk * LANES, (chunk + 1) * LANES)
        write(chunk * 8, 8, rows[:main, lanes].reshape(groups, 8, LANES).astype(BF16))
        overflow[:, chunk, :] = rows[main:, lanes]
    write(64, 16, overflow[...].reshape(groups, 16, LANES).astype(BF16))


def route_kernel(ids_ref, place_ref):
    expert = lax.broadcasted_iota(jnp.int32, (EXPERTS, 128), 0)
    first = ids_ref[0:1, :]
    second = ids_ref[1:2, :]
    one = jnp.ones((EXPERTS, 128), F32)
    zero = jnp.zeros((EXPERTS, 128), F32)
    named = jnp.where(expert == first, one, zero) + jnp.where(expert == second, one, zero)
    earlier = lax.broadcasted_iota(jnp.int32, (128, 128), 0) < lax.broadcasted_iota(
        jnp.int32, (128, 128), 1
    )
    earlier = jnp.where(earlier, jnp.ones((128, 128), F32), jnp.zeros((128, 128), F32))
    before = dot_nn(named.astype(BF16), earlier.astype(BF16))
    for row, chosen in enumerate((first, second)):
        slot = jnp.sum(jnp.where(expert == chosen, before, zero), axis=0, keepdims=True)
        slot = slot.astype(jnp.int32)
        over = EXPERTS * MAIN + chosen * (CAP - MAIN) + slot - MAIN
        place_ref[row : row + 1, :] = jnp.where(slot < MAIN, chosen * MAIN + slot, over)


def picks(place_ref):
    slot = lax.broadcasted_iota(jnp.int32, (EXPERTS * CAP, 128), 0)
    return slot == place_ref[0:1, :], slot == place_ref[1:2, :]


def selection(first, second):
    zero = jnp.zeros((EXPERTS * CAP, 128), F32)
    return (jnp.where(first, 1.0, zero) + jnp.where(second, 1.0, zero)).astype(BF16)


def into(block_ref):
    def put(start, size, block):
        block_ref[:, start : start + size, :] = block

    return put


def start_all(copies):
    for copy in copies:
        copy.start()
    return copies


def send_twice(block_ref, send_ref, sems):
    return start_all(
        [pltpu.make_async_copy(block_ref, send_ref.at[:, copy], sems.at[copy]) for copy in (0, 1)]
    )


def grads_kernel(place_ref, gate_ref, rows_ref, send_ref, overflow, block, sems):
    first, second = picks(place_ref)
    zero = jnp.zeros((EXPERTS * CAP, 128), F32)
    gate = jnp.where(first, gate_ref[0:1, :], zero) + jnp.where(second, gate_ref[1:2, :], zero)
    gate = jnp.sum(gate, axis=1, keepdims=True)
    cotangent = rows_ref[:, 8:16, :].astype(F32).reshape(128, 1024).astype(BF16)
    grads = gate * dot_nn(selection(first, second), cotangent)
    pack_blocks(grads, overflow, EXPERTS, into(block))
    for copy in send_twice(block, send_ref, sems):
        copy.wait()


def forward_kernel(
    device_ref,
    place_ref,
    rows_ref,
    *refs,
):
    pieces, refs = refs[:10], refs[10:]
    send_ref, query_ref, key_ref, value_ref, probs_ref, mid_ref, *refs = refs
    weights, overflow, query, key, value, probabilities, middle, send, sems, out_sems = refs
    copies = weight_copies(device_ref, pieces, weights, sems)
    for pair in copies:
        for copy in pair:
            copy.start()
    low = lane_halves()
    fields = rows_ref[:, 0:8, :].astype(F32).reshape(128, 1024)
    normed, _ = normalize(fields)
    normed = normed.astype(BF16)
    leaving = []
    for which, (held, out) in enumerate(
        ((query, query_ref), (key, key_ref), (value, value_ref))
    ):
        wait_for(copies, which)
        held[...] = dot_nn(normed, whole(weights, which)).astype(BF16)
        leaving += start_all([pltpu.make_async_copy(held, out, out_sems.at[which])])
    attended = []
    for block in range(8):
        lanes = slice(block * LANES, (block + 1) * LANES)
        scores = dot_nt(query[:, lanes], split_heads(key[:, lanes], low)) * 0.125
        parts = []
        for half in range(2):
            part = scores[:, half * LANES : (half + 1) * LANES]
            part = jnp.exp(part - jnp.max(part, axis=-1, keepdims=True))
            parts.append(part / jnp.sum(part, axis=-1, keepdims=True))
        probs = jnp.concatenate(parts, axis=1)
        probabilities[block] = probs
        attended.append(dot_nn(probs.astype(BF16), split_heads(value[:, lanes], low)).astype(BF16))
    leaving += start_all([pltpu.make_async_copy(probabilities, probs_ref, out_sems.at[3])])
    wait_for(copies, 3)
    mixture = dot_nn(jnp.concatenate(attended, axis=1), whole(weights, 3))
    mid = (fields + mixture).astype(BF16)
    middle[...] = mid
    leaving += start_all([pltpu.make_async_copy(middle, mid_ref, out_sems.at[4])])
    normed_mid, _ = normalize(mid.astype(F32))
    inputs = dot_nn(selection(*picks(place_ref)), normed_mid.astype(BF16))
    pack_blocks(inputs, overflow, EXPERTS, into(send))
    leaving += send_twice(send, send_ref, out_sems.at[5:7])
    for copy in leaving:
        copy.wait()


def unpack_into(source, out_ref, overflow):
    overflow[...] = source[:, 64:80, :].astype(F32).reshape(128, 8, LANES)
    for chunk in range(8):
        lanes = slice(chunk * LANES, (chunk + 1) * LANES)
        tile = source[:, chunk * 8 : chunk * 8 + 8, :]
        out_ref[0:512, lanes] = tile.astype(F32).reshape(512, LANES).astype(BF16)
        out_ref[512:640, lanes] = overflow[:, chunk, :].astype(BF16)


def expert_kernel(
    source_ref,
    act_grad_ref,
    gate_ref,
    up_ref,
    inputs_ref,
    hidden_ref,
    gate_delta_ref,
    up_delta_ref,
    back_ref,
    source,
    act_grads,
    gates,
    ups,
    inputs,
    hidden,
    gate_delta,
    up_delta,
    back,
    overflow,
    sems,
    out_sems,
):
    parts = [slice(part * 256, (part + 1) * 256) for part in range(4)]
    first = pltpu.make_async_copy(source_ref, source, sems.at[0, 3])
    first.start()
    entering = [
        start_all(
            [
                pltpu.make_async_copy(whole_ref.at[:, units], held.at[:, units], sems.at[part, k])
                for k, (whole_ref, held) in enumerate(
                    ((gate_ref, gates), (up_ref, ups), (act_grad_ref, act_grads))
                )
            ]
        )
        for part, units in enumerate(parts)
    ]
    first.wait()
    unpack_into(source, inputs, overflow)
    leaving = start_all([pltpu.make_async_copy(inputs, inputs_ref, out_sems.at[0, 3])])
    rows = inputs[...]
    for part, units in enumerate(parts):
        for copy in entering[part]:
            copy.wait()
        gate_pre = dot_nn(rows, gates[:, units])
        up_pre = dot_nn(rows, ups[:, units])
        sigmoid_gate = jax.nn.sigmoid(gate_pre)
        swish_gate = gate_pre * sigmoid_gate
        act_grad = act_grads[:, units]
        hidden[:, units] = (swish_gate * up_pre).astype(BF16)
        slope = sigmoid_gate * (1.0 + gate_pre * (1.0 - sigmoid_gate))
        gate_delta[:, units] = (act_grad * up_pre * slope).astype(BF16)
        up_delta[:, units] = (act_grad * swish_gate).astype(BF16)
        leaving += start_all(
            [
                pltpu.make_async_copy(
                    held.at[:, units], out.at[:, units], out_sems.at[part, k]
                )
                for k, (held, out) in enumerate(
                    ((hidden, hidden_ref), (gate_delta, gate_delta_ref), (up_delta, up_delta_ref))
                )
            ]
        )
    for part in range(2):
        rows = slice(part * 320, (part + 1) * 320)
        total = dot_nt(gate_delta[rows, :], gates[...]) + dot_nt(up_delta[rows, :], ups[...])
        back[rows, :] = total.astype(back.dtype)
        leaving += start_all(
            [pltpu.make_async_copy(back.at[rows], back_ref.at[rows], out_sems.at[1 + part, 3])]
        )
    for copy in leaving:
        copy.wait()


def return_kernel(own_ref, other_ref, send_ref, overflow):
    def put(start, size, block):
        send_ref[:, start : start + size, :] = block

    pack_blocks(own_ref[...].astype(F32) + other_ref[...].astype(F32), overflow, 64, put)


def backward_kernel(device_ref, place_ref, back_ref, rows_ref, *refs):
    stored, pieces, refs = refs[:5], refs[5:15], refs[15:]
    out_ref, weights, returned, overflow, grad_query, grad_key, grad_value, *refs = refs
    held, sems, in_sems = refs[:5], refs[5], refs[6]
    query_ref, key_ref, value_ref, probs_ref, mid_ref = held
    copies = weight_copies(device_ref, pieces, weights, sems)
    entering = [
        pltpu.make_async_copy(source, target, in_sems.at[which])
        for which, (source, target) in enumerate(zip(stored, held))
    ]
    entering[4].start()
    start_all(copies[3])
    for which in (2, 3, 1, 0):
        entering[which].start()
    for which in (0, 1, 2):
        start_all(copies[which])
    low = lane_halves()
    for copy in range(2):
        start = copy * 320
        overflow[...] = back_ref[:, copy, 64:80, :].astype(F32).reshape(64, 8, LANES)
        for chunk in range(8):
            lanes = slice(chunk * LANES, (chunk + 1) * LANES)
            tile = back_ref[:, copy, chunk * 8 : chunk * 8 + 8, :]
            returned[start : start + 256, lanes] = (
                tile.astype(F32).reshape(256, LANES).astype(BF16)
            )
            returned[start + 256 : start + 320, lanes] = overflow[:, chunk, :].astype(BF16)
    select = selection(*picks(place_ref))
    normed_grad = dot_tn(select, returned[0:320, :]) + dot_tn(select, returned[320:640, :])
    entering[4].wait()
    normed_mid, scale_mid = normalize(mid_ref[...].astype(F32))
    cotangent = rows_ref[:, 8:16, :].astype(F32).reshape(128, 1024)
    block_grad = cotangent + norm_back(normed_grad, normed_mid, scale_mid)
    wait_for(copies, 3)
    out_grad = dot_nt(block_grad.astype(BF16), whole(weights, 3)).astype(BF16)
    for which in range(4):
        entering[which].wait()
    for block in range(8):
        lanes = slice(block * LANES, (block + 1) * LANES)
        outs = out_grad[:, lanes]
        probs = probs_ref[block]
        mass = probs * dot_nt(outs, split_heads(value_ref[:, lanes], low))
        parts = []
        for half in range(2):
            part = slice(half * LANES, (half + 1) * LANES)
            total = jnp.sum(mass[:, part], axis=-1, keepdims=True)
            parts.append((mass[:, part] - probs[:, part] * total) * 0.125)
        score_grad = jnp.concatenate(parts, axis=1).astype(BF16)
        grad_query[:, lanes] = dot_nn(score_grad, split_heads(key_ref[:, lanes], low)).astype(BF16)
        keys = dot_tn(score_grad, query_ref[:, lanes])
        grad_key[:, lanes] = jnp.where(low, keys[0:128], keys[128:256]).astype(BF16)
        values = dot_tn(probs.astype(BF16), outs)
        grad_value[:, lanes] = jnp.where(low, values[0:128], values[128:256]).astype(BF16)
    wait_for(copies, 0)
    branch = dot_nt(grad_query[...], whole(weights, 0))
    wait_for(copies, 1)
    branch = branch + dot_nt(grad_key[...], whole(weights, 1))
    wait_for(copies, 2)
    branch = branch + dot_nt(grad_value[...], whole(weights, 2))
    fields = rows_ref[:, 0:8, :].astype(F32).reshape(128, 1024)
    normed, scale = normalize(fields)
    total = block_grad + norm_back(branch, normed, scale)
    out_ref[...] = total.reshape(16, 8, 1024).astype(BF16)


def shape(*dims, dtype=BF16):
    return jax.ShapeDtypeStruct(dims, dtype)


def route(ids):
    return pl.pallas_call(
        route_kernel,
        out_shape=shape(2, 128, dtype=jnp.int32),
        in_specs=[IN_VMEM],
        out_specs=IN_VMEM,
        compiler_params=grant(2),
        name="route",
    )(ids)


def dispatch_grads(places, gates, rows):
    return pl.pallas_call(
        grads_kernel,
        out_shape=shape(EXPERTS, 2, 80, LANES),
        in_specs=[IN_VMEM, IN_VMEM, IN_VMEM],
        out_specs=IN_HBM,
        scratch_shapes=[
            pltpu.VMEM((64, 8, LANES), F32),
            pltpu.VMEM((EXPERTS, 80, LANES), BF16),
            pltpu.SemaphoreType.DMA((2,)),
        ],
        compiler_params=grant(8),
        name="dispatch_grads",
    )(places, gates, rows)


STORED = (
    (128, 1024, BF16),
    (128, 1024, BF16),
    (128, 1024, BF16),
    (8, 128, 256, F32),
    (128, 1024, BF16),
)
HELD = [pltpu.VMEM(tuple(dims), kind) for *dims, kind in STORED]
WEIGHTS = pltpu.VMEM((4, 64, 2, 8, 1024), BF16)


def forward(device, places, rows, pieces):
    return pl.pallas_call(
        forward_kernel,
        out_shape=(shape(EXPERTS, 2, 80, LANES),)
        + tuple(shape(*dims, dtype=kind) for *dims, kind in STORED),
        in_specs=[IN_SMEM, IN_VMEM, IN_VMEM] + [IN_HBM] * 10,
        out_specs=tuple([IN_HBM] * 6),
        scratch_shapes=[WEIGHTS, pltpu.VMEM((64, 8, LANES), F32)]
        + HELD
        + [
            pltpu.VMEM((EXPERTS, 80, LANES), BF16),
            pltpu.SemaphoreType.DMA((4, 4)),
            pltpu.SemaphoreType.DMA((7,)),
        ],
        compiler_params=grant(60),
        name="forward",
    )(device, places, rows, *pieces)


def unpack(source):
    return pl.pallas_call(
        unpack_into,
        out_shape=shape(640, 1024),
        in_specs=[IN_VMEM],
        out_specs=IN_VMEM,
        scratch_shapes=[pltpu.VMEM((128, 8, LANES), F32)],
        compiler_params=grant(8),
        name="unpack",
    )(source)


def expert_half(source, act_grad, gate_block, up_block, kind):
    half = pltpu.VMEM((640, 1024), BF16)
    square = pltpu.VMEM((1024, 1024), BF16)
    return pl.pallas_call(
        expert_kernel,
        out_shape=tuple([shape(640, 1024)] * 4) + (shape(640, 1024, dtype=kind),),
        in_specs=[IN_HBM] * 4,
        out_specs=tuple([IN_HBM] * 5),
        scratch_shapes=[pltpu.VMEM((64, 80, LANES), BF16), pltpu.VMEM((640, 1024), F32)]
        + [square, square, half, half, half, half, pltpu.VMEM((640, 1024), kind)]
        + [
            pltpu.VMEM((128, 8, LANES), F32),
            pltpu.SemaphoreType.DMA((4, 4)),
            pltpu.SemaphoreType.DMA((4, 4)),
        ],
        compiler_params=grant(60),
        cost_estimate=pl.CostEstimate(
            flops=8 * 640 * 1024 * 1024, bytes_accessed=12 << 20, transcendentals=640 * 1024
        ),
        name="expert_half",
    )(source, act_grad, gate_block, up_block)


def pack_return(own, other):
    return pl.pallas_call(
        return_kernel,
        out_shape=shape(64, 80, LANES),
        in_specs=[IN_VMEM, IN_VMEM],
        out_specs=IN_VMEM,
        scratch_shapes=[pltpu.VMEM((128, 8, LANES), F32)],
        compiler_params=grant(8),
        name="pack_return",
    )(own, other)


def backward(device, places, back, rows, pieces, stored):
    return pl.pallas_call(
        backward_kernel,
        out_shape=shape(16, 8, 1024),
        in_specs=[IN_SMEM] + [IN_VMEM] * 3 + [IN_HBM] * 15,
        out_specs=IN_VMEM,
        scratch_shapes=[
            WEIGHTS,
            pltpu.VMEM((640, 1024), BF16),
            pltpu.VMEM((64, 8, LANES), F32),
            pltpu.VMEM((128, 1024), BF16),
            pltpu.VMEM((128, 1024), BF16),
            pltpu.VMEM((128, 1024), BF16),
        ]
        + HELD
        + [pltpu.SemaphoreType.DMA((4, 4)), pltpu.SemaphoreType.DMA((5,))],
        compiler_params=grant(BACKWARD_GRANT),
        name="backward",
    )(device, places, back, rows, *stored, *pieces)


def exchange(blocks, axes):
    return lax.all_to_all(blocks, axes, split_axis=0, concat_axis=0, tiled=True)


PAIRS_OF_FOUR = [(0, 1), (1, 0), (2, 3), (3, 2)]
NEIGHBOURS = (
    ("xl", SWAP),
    ("y", PAIRS_OF_FOUR),
    ("z", PAIRS_OF_FOUR),
    (("xh", "xl"), [(0, 3), (3, 0), (1, 2), (2, 1)]),
)


def gather_weights(shards):
    halves = [shard.reshape(8, 2, 512).transpose(1, 0, 2) for shard in shards]
    sides = [halves[0], jnp.tile(halves[1], (2, 1, 1)), jnp.tile(halves[2], (2, 1, 1)), halves[3]]
    spread = [
        jnp.broadcast_to(jnp.expand_dims(side, axes), (2, 4, 4, 2, 8, 512))
        for side, axes in zip(sides, ((0, 1, 2), (0, 2, 3), (0, 1, 3), (0, 1, 2)))
    ]
    arrived = exchange(jnp.stack(spread, axis=4).reshape(64, 4, 8, 512), SAME_CORE)
    arrived_other = lax.ppermute(arrived, "core", SWAP)
    own, other = [arrived], [arrived_other]
    for which, (axes, pairs) in enumerate(NEIGHBOURS):
        piece = lax.ppermute(arrived[:, which], axes, pairs)
        own.append(piece)
        other.append(lax.ppermute(piece, "core", SWAP))
    return own + other


def block_backward(
    fields,
    cotangent,
    query_weight,
    key_weight,
    value_weight,
    output_weight,
    expert_ids,
    gate_values,
    gate_weight,
    up_weight,
    down_weight,
):
    gate_block, up_block, down_block = gate_weight[0], up_weight[0], down_weight[0]
    pieces = gather_weights([query_weight, key_weight, value_weight, output_weight])
    rows = exchange(jnp.concatenate([fields, cotangent], axis=1), COL)
    device = jnp.stack(
        [
            lax.axis_index("core"),
            lax.axis_index("xl"),
            lax.axis_index("y") % 2,
            lax.axis_index("z") % 2,
        ]
    ).astype(jnp.int32)
    places = route(expert_ids.reshape(128, 2).T)
    gates = gate_values.reshape(128, 2).T
    grads_out = dispatch_grads(places, gates, rows)
    grads_own = exchange(grads_out.reshape(64, 80, LANES), SAME_CORE)
    grads_other = lax.ppermute(grads_own, "core", SWAP)
    inputs_out, *stored = forward(device, places, rows, pieces)
    inputs_own = exchange(inputs_out.reshape(64, 80, LANES), SAME_CORE)
    inputs_other = lax.ppermute(inputs_own, "core", SWAP)
    halves = []
    for gradients, inputs, kind in (
        (grads_other, inputs_other, BF16), (grads_own, inputs_own, F32)
    ):
        gradients = unpack(gradients)
        act_grad = dot_nt(gradients, down_block)
        terms = expert_half(inputs, act_grad, gate_block, up_block, kind)
        halves.append((gradients, *terms))
    away = lax.ppermute(halves[0][-1], "core", SWAP)
    send_back = pack_return(halves[1][-1], away)
    grads, inputs, hidden, gate_delta, up_delta, _ = zip(*halves)
    send_back, gate_delta, hidden = lax.optimization_barrier((send_back, gate_delta, hidden))
    back = exchange(send_back, SAME_CORE)

    def grad(left, right):
        return (dot_tn(left[0], right[0]) + dot_tn(left[1], right[1])).astype(BF16)[None]

    gate_term = grad(inputs, gate_delta)
    down_term = grad(hidden, grads)
    field_half = backward(device, places, back.reshape(EXPERTS, 2, 80, LANES), rows, pieces, stored)
    field_half, up_delta = lax.optimization_barrier((field_half, up_delta))
    field_grad = exchange(field_half, COL)
    up_term = grad(inputs, up_delta)
    return (field_grad, gate_term, up_term, down_term)


def solution(mesh):
    fine = jax.sharding.Mesh(mesh.devices.reshape(2, 4, 4, 2, 2), EVERY)
    in_specs = (
        P(ROW, COL, None),
        P(ROW, COL, None),
        P(EVERY, None),
        P(EVERY, None),
        P(EVERY, None),
        P(EVERY, None),
        P(ROW, COL, None, None),
        P(ROW, COL, None, None),
        P(EVERY, None, None),
        P(EVERY, None, None),
        P(EVERY, None, None),
    )
    out_specs = (
        P(ROW, COL, None),
        P(EVERY, None, None),
        P(EVERY, None, None),
        P(EVERY, None, None),
    )
    return jax.shard_map(block_backward, mesh=fine, in_specs=in_specs, out_specs=out_specs, check_vma=False)
```
